32 devices in a mesh: grp: 2 (over y), freq: 4 (over z), ell: 2 (over x), pol: 2 (over core).
Axes of the slice: x: 2, y: 2, z: 4, core: 2. Of those that a mesh axis runs over, the one named last changes fastest.
Arguments:
- beam_matrix: bfloat16 [8, 2, 512, 8192], P(('grp', 'freq'), None, None, ('ell', 'pol')), parts along dimension 0, may hold values from -0.375 to 0.375
- sky_spectrum: float32 [8, 3, 8192], P(('grp', 'freq'), None, ('ell', 'pol')), parts along dimension 0, may hold values from 0.1 to 10
- taper_tiles: bfloat16 [3, 512, 512], P(None, ('ell', 'pol')), may hold values from 0.5 to 1.5
- noise_tiles: bfloat16 [8, 3, 512, 2, 512], P(('grp', 'freq'), None, ('ell', 'pol')), parts along dimension 0, may hold values from -4 to 4
Outputs:
- covariance: float32 [8, 3, 512, 2, 512], P(('grp', 'freq'), None, ('ell', 'pol')), parts along dimension 0
The draws below stay inside these ranges and needn't reach their ends.
There are 2 independent parts, one for each index of `grp`. The reference program is written for one: setup_inputs(seed, part) draws one part's arguments, and reference() takes and returns one part's arrays. A program takes and returns all parts, laid end to end along the dimension named above; an argument that names none is the same for every part. Nothing has to cross between parts.
All inputs are finite; a program needn't handle non-finite values.
Results may differ from the reference program's by a relative error of at most 0.012.
Values may be sent and summed in bfloat16 or wider, within the bound.
A program may use at most 64 MiB of HBM per device.

```python
import math
import jax
import jax.numpy as jnp
from jax import lax

MODES = 512
LPOL = 8192
SEPS = 3
NFREQ = 4
N_ELL = 2
N_POL = 2


def raised(array, key, source, target, blocks, factor):
    def block_of(position):
        return (jnp.arange(array.shape[position]) // (array.shape[position] // blocks)).reshape((-1,) + (1,) * (array.ndim - 1 - position))

    near = jax.random.permutation(key, blocks)[block_of(target)]
    other_side = (block_of(target) + blocks // 2) % blocks
    return jnp.where((block_of(source) == near) | (block_of(source) == other_side), factor * array, array)


def block_levels(stream_key, dims, pieces, low, top_value):
    factor_of, own = 1.0, jax.random.fold_in(stream_key, 6)
    for position, parts in pieces:
        draws = jnp.exp(jax.random.uniform(jax.random.fold_in(own, position), (parts,), jnp.float32, low / len(pieces), top_value / len(pieces)))
        factor_of = factor_of * jnp.repeat(draws, dims[position] // parts).reshape([-1 if axis == position else 1 for axis in range(len(dims))])
    return factor_of


def centred(rng, dims, deviation, most, cuts=(), held_as=jnp.bfloat16):
    loudness = block_levels(rng, dims, cuts, -0.22, 0.18) if cuts else 1.0
    values = jax.random.normal(rng, dims, jnp.float32) * deviation * loudness
    return jnp.minimum(jnp.maximum(values, -most), most).astype(held_as)


def bell_draw_with(rng, extent, deviation, reach, cuts, heavy, held_as=jnp.bfloat16):
    drawn = deviation * jax.random.normal(rng, extent, jnp.float32)
    if cuts:
        drawn = drawn * block_levels(rng, extent, cuts, -0.22, 0.18)
    return jnp.clip(raised(drawn, jax.random.fold_in(rng, 3), *heavy), -reach, reach).astype(held_as)


def setup_inputs(seed: int = 0, part: int = 0) -> dict:
    keys = jax.random.split(jax.random.key(seed), 5)
    part_splits = jax.random.split(jax.random.fold_in(keys[4], part), 5)
    beam_matrix = bell_draw_with(part_splits[0], (NFREQ, 2, MODES, LPOL), (LPOL // 16) ** -0.5, 0.375, ((0, 4), (3, 4)), (3, 2, 4, 2.0))
    sky_spectrum = jnp.clip(jnp.exp(math.log(10.0) - 4.6051702 * jax.random.uniform(part_splits[1], (NFREQ, SEPS, LPOL), jnp.float32) ** block_levels(part_splits[1], (NFREQ, SEPS, LPOL), ((0, 4), (2, 4)), -0.2, 0.2)), 0.1, 10.0)
    taper_tiles = jnp.clip(0.5 + 1.0 * jax.random.uniform(keys[2], (SEPS, MODES, MODES), jnp.float32) ** block_levels(keys[2], (SEPS, MODES, MODES), ((1, 4),), -0.2, 0.2), 0.5, 1.5).astype(jnp.bfloat16)
    noise_tiles = centred(part_splits[3], (NFREQ, SEPS, MODES, 2, MODES), 0.5, 4.0, ((0, 4), (2, 4)))
    return dict(beam_matrix=beam_matrix, sky_spectrum=sky_spectrum, taper_tiles=taper_tiles, noise_tiles=noise_tiles)


def tile_sum(own_beam, spec_row, partner):
    mode_count = own_beam.shape[1]
    multipoles = own_beam.shape[2]
    group_count = N_ELL * N_POL
    group_width = multipoles // group_count
    scaled = (spec_row[None, None, :] * own_beam.astype(jnp.float32)).astype(jnp.bfloat16)
    scaled = lax.optimization_barrier(scaled)
    left_wide = scaled.astype(jnp.float32).reshape(2, mode_count, group_count, group_width)
    right_wide = partner.astype(jnp.float32).reshape(2, mode_count, group_count, group_width)
    real_part = jnp.einsum("mgl,ngl->gmn", left_wide[0], right_wide[0]) + jnp.einsum("mgl,ngl->gmn", left_wide[1], right_wide[1])
    imag_part = jnp.einsum("mgl,ngl->gmn", left_wide[1], right_wide[0]) - jnp.einsum("mgl,ngl->gmn", left_wide[0], right_wide[1])
    partials = jnp.stack([real_part, imag_part], axis=2).astype(jnp.bfloat16)
    partials = lax.optimization_barrier(partials)
    return jnp.sum(partials.astype(jnp.float32), axis=0)


def reference(beam_matrix, sky_spectrum, taper_tiles, noise_tiles):
    freq_total = beam_matrix.shape[0]

    def one_freq(bundle):
        own_beam, spec_rows, noise_rows, freq_index = bundle
        per_sep = []
        for sep_index in range(SEPS):
            target = freq_index + sep_index + 1
            picked = jnp.minimum(target, freq_total - 1).astype(jnp.int32)
            partner = lax.dynamic_index_in_dim(beam_matrix, picked, 0, keepdims=False)
            partner = jnp.where(target < freq_total, partner, jnp.zeros_like(partner))
            summed = tile_sum(own_beam, spec_rows[sep_index], partner)
            per_sep.append(taper_tiles[sep_index].astype(jnp.float32)[:, None, :] * summed + noise_rows[sep_index].astype(jnp.float32))
        return jnp.stack(per_sep)

    indices = jnp.arange(freq_total, dtype=jnp.int32)
    return lax.map(one_freq, (beam_matrix, sky_spectrum, noise_tiles, indices))
```

```python
import functools

import jax
import jax.numpy as jnp
from jax import lax
from jax.experimental import pallas as pl
from jax.experimental.pallas import tpu as pltpu
from jax.sharding import PartitionSpec as P

CHUNKS = 4
LANES = 128


def passed_along(block, axis, distance):
    devices = range(lax.axis_size(axis))
    route = [(i - distance, i) for i in devices if i - distance in devices]
    return lax.ppermute(block, axis, route)


def general_sums(beam_matrix, sky_spectrum, local_rows):
    per_device = beam_matrix.shape[0]
    mode_count = beam_matrix.shape[2]
    separations = sky_spectrum.shape[1]
    needed = (per_device - 1 + separations) // per_device
    blocks = [beam_matrix]
    for offset in range(needed):
        blocks.append(passed_along(beam_matrix, "freq", -(offset + 1)))
    term_list = []
    for sep_index in range(separations):
        target = sep_index + 1
        partner = blocks[target // per_device][target % per_device]
        spec_row = sky_spectrum[0, sep_index]
        scaled = (spec_row[None, None, :] * beam_matrix[0].astype(jnp.float32)).astype(jnp.bfloat16)
        right = jnp.concatenate([partner[0], partner[1]], axis=-1)
        top = jnp.concatenate([scaled[0], scaled[1]], axis=-1)
        bottom = jnp.concatenate([scaled[1], -scaled[0]], axis=-1)
        left = jnp.stack([top, bottom], axis=1).reshape(2 * mode_count, top.shape[-1])
        product = lax.dot_general(
            left, right, (((1,), (1,)), ((), ())), preferred_element_type=jnp.float32
        ).reshape(mode_count, 2, mode_count)
        term_list.append(
            lax.psum_scatter(
                product.astype(jnp.bfloat16), ("ell", "pol"), scatter_dimension=0, tiled=True
            ).astype(jnp.float32)
        )
    return jnp.stack(term_list)


T12, T13, T02, T03, TEND = range(5)


def meet_kernel(
    cut, own, spec, out,
    outer, near, far, spec0, spec1, stage, inbox, back_out, back_in, final_out, final_in,
    spec_s, spec_r, near_s, near_r, o1_s, o1_r, o2_s, o2_r, fw_s, fw_r,
    rs_s, rs_r, bk_s, bk_r, fn_s, fn_r,
):
    f32, bf16 = jnp.float32, jnp.bfloat16
    _, groups, rows, width = own.shape
    modes = groups * rows
    chunks = CHUNKS
    step = rows // chunks
    freqs = lax.axis_size("freq")
    pols = lax.axis_size("pol")
    freq = lax.axis_index("freq")
    me = lax.axis_index("ell") * pols + lax.axis_index("pol")
    low, high, full = (0, cut), (cut, width), (0, width)
    every = slice(None)

    barrier = pltpu.get_barrier_semaphore()
    for d in range(1, freqs):
        pl.semaphore_signal(
            barrier, inc=1, device_id={"freq": lax.rem(freq + d, freqs)},
            device_id_type=pl.DeviceIdType.MESH,
        )
    for d in range(1, groups):
        other = lax.rem(me + d, groups)
        pl.semaphore_signal(
            barrier, inc=1, device_id={"ell": other // pols, "pol": lax.rem(other, pols)},
            device_id_type=pl.DeviceIdType.MESH,
        )
    pl.semaphore_wait(barrier, freqs - 1 + groups - 1)

    def span(c):
        return pl.ds(pl.multiple_of(c * step, step), step)

    def to_freq(src, dst, send, recv, target):
        return pltpu.make_async_remote_copy(
            src_ref=src, dst_ref=dst, send_sem=send, recv_sem=recv,
            device_id={"freq": target}, device_id_type=pl.DeviceIdType.MESH,
        )

    def lanes(part):
        return pl.ds(part[0], part[1] - part[0])

    def send_spec(n, src, dst, target):
        return to_freq(src, dst, spec_s.at[n], spec_r.at[n], target)

    def mid(part, target):
        where = (every, every, every, lanes(part))
        return to_freq(own.at[where], near.at[where], near_s.at[0], near_r.at[0], target)

    def row_chunk(c, part):
        return (every, every, span(c), lanes(part))

    def block_chunk(g, part):
        return (every, pl.ds(g, 1), every, lanes(part))

    def hop(src, dst, send, recv, c, where, target):
        return to_freq(src.at[where], dst.at[where], send.at[c], recv.at[c], target)

    def share(tile, piece, where):
        copies = []
        for d in range(1, groups):
            other = lax.rem(me + d, groups)
            copies.append(
                pltpu.make_async_remote_copy(
                    src_ref=stage.at[(tile, other) + where],
                    dst_ref=inbox.at[(tile, d - 1) + where],
                    send_sem=rs_s.at[tile, piece, d - 1],
                    recv_sem=rs_r.at[tile, piece, d - 1],
                    device_id={"ell": other // pols, "pol": lax.rem(other, pols)},
                    device_id_type=pl.DeviceIdType.MESH,
                )
            )
        return copies

    def start_share(tile, piece, where):
        for copy in share(tile, piece, where):
            copy.start()

    whole = (every, every, every)

    def rows_of(c):
        return (every, span(c), every)

    def cols_of(g):
        return (every, every, pl.ds(pl.multiple_of(g * rows, rows), rows))

    def dot(a, b):
        return lax.dot_general(a, b, (((1,), (1,)), ((), ())), preferred_element_type=f32)

    def scaled(block, part_index, where, weight):
        value = block[(part_index,) + where].reshape(-1, weight.shape[-1])
        return (weight * value.astype(f32)).astype(bf16)

    def cross(left, left_where, weight, right, right_where):
        a_re = scaled(left, 0, left_where, weight)
        a_im = scaled(left, 1, left_where, weight)
        b_re = right[(0,) + right_where].reshape(-1, weight.shape[-1])
        b_im = right[(1,) + right_where].reshape(-1, weight.shape[-1])
        real = dot(a_re, b_re) + dot(a_im, b_im)
        imag = dot(a_im, b_re) - dot(a_re, b_im)
        return real.astype(bf16), imag.astype(bf16)

    def by_rows(tile, c, left, weights, sep, right, part):
        weight = weights[pl.ds(sep, 1), lanes(part)]
        real, imag = cross(
            left, (every, span(c), lanes(part)), weight, right, (every, every, lanes(part))
        )
        stage[tile, :, 0, span(c), :] = real.reshape(groups, step, modes)
        stage[tile, :, 1, span(c), :] = imag.reshape(groups, step, modes)

    def by_columns(tile, g, left, weights, sep, right, part):
        weight = weights[pl.ds(sep, 1), lanes(part)]
        columns = pl.ds(pl.multiple_of(g * rows, rows), rows)

        def body(o, carry):
            real, imag = cross(
                left, (o, every, lanes(part)), weight, right, (g, every, lanes(part))
            )
            stage[tile, o, 0, :, columns] = real
            stage[tile, o, 1, :, columns] = imag
            return carry

        lax.fori_loop(0, groups, body, 0)

    def gathered(tile, piece, where):
        for copy in share(tile, piece, where):
            copy.wait_recv()
        total = stage[(tile, me) + where].astype(f32)
        for d in range(groups - 1):
            total = total + inbox[(tile, d) + where].astype(f32)
        return total

    def loop(lo, hi, body):
        def wrapped(i, carry):
            body(i)
            return carry

        lax.fori_loop(lo, hi, wrapped, 0)

    def settle(tile, pieces, where_of):
        def body(c):
            for copy in share(tile, c, where_of(c)):
                copy.wait_send()

        loop(0, pieces, body)

    def give_back(tile, c, where):
        return to_freq(
            back_out.at[(tile,) + where], back_in.at[(tile,) + where],
            bk_s.at[tile, c], bk_r.at[tile, c], 1,
        )

    def deliver(sep, c):
        where = rows_of(c)
        return to_freq(
            final_out.at[(sep,) + where], final_in.at[(sep,) + where],
            fn_s.at[sep, c], fn_r.at[sep, c], 0,
        )

    @pl.when(freq == 0)
    def _():
        send_spec(0, spec, spec0, 1).start()
        send_spec(1, spec, spec0, 2).start()
        loop(0, chunks, lambda c: hop(own, outer, o1_s, o1_r, c, row_chunk(c, high), 1).start())
        loop(0, chunks, lambda c: hop(own, outer, o2_s, o2_r, c, row_chunk(c, low), 1).start())
        send_spec(0, spec, spec0, 1).wait_send()
        send_spec(1, spec, spec0, 2).wait_send()
        loop(0, chunks, lambda c: hop(own, outer, o1_s, o1_r, c, row_chunk(c, high), 1).wait_send())
        loop(0, chunks, lambda c: hop(own, outer, o2_s, o2_r, c, row_chunk(c, low), 1).wait_send())
        for sep in range(3):
            loop(0, chunks, lambda c: deliver(sep, c).wait_recv())
            out[sep] = final_in[sep]

    @pl.when(freq == 3)
    def _():
        loop(0, groups, lambda g: hop(own, outer, o1_s, o1_r, g, block_chunk(g, low), 2).start())
        loop(0, groups, lambda g: hop(own, outer, o2_s, o2_r, g, block_chunk(g, high), 2).start())
        out[...] = jnp.zeros_like(out)
        loop(0, groups, lambda g: hop(own, outer, o1_s, o1_r, g, block_chunk(g, low), 2).wait_send())
        loop(0, groups, lambda g: hop(own, outer, o2_s, o2_r, g, block_chunk(g, high), 2).wait_send())

    @pl.when(freq == 1)
    def _():
        send_spec(2, spec, spec1, 2).start()
        mid(high, 2).start()

        def relay(c):
            hop(own, outer, o1_s, o1_r, c, row_chunk(c, high), 1).wait_recv()
            hop(outer, far, fw_s, fw_r, c, row_chunk(c, high), 2).start()

        loop(0, chunks - 1, relay)
        mid(low, 1).wait_recv()
        loop(0, chunks, lambda c: by_rows(T12, c, own, spec, 0, near, low))
        start_share(T12, 0, whole)
        loop(chunks - 1, chunks, relay)
        send_spec(0, spec, spec0, 1).wait_recv()

        def finish_end(c):
            final_out[(0,) + rows_of(c)] = gathered(TEND, c, rows_of(c)).astype(bf16)
            deliver(0, c).start()

        def take(c):
            hop(own, outer, o2_s, o2_r, c, row_chunk(c, low), 1).wait_recv()
            by_rows(TEND, c, outer, spec0, 0, own, full)
            start_share(TEND, c, rows_of(c))
            by_rows(T02, c, outer, spec0, 1, near, low)
            start_share(T02, c, rows_of(c))

            @pl.when(c == chunks - 2)
            def _():
                loop(0, groups, lambda g: hop(
                    outer, far, fw_s, fw_r, g, block_chunk(g, low), 1).wait_recv())
                loop(0, chunks, lambda r: by_rows(T13, r, own, spec, 1, far, low))
                start_share(T13, 0, whole)

            def last(r):
                by_rows(T03, r, outer, spec0, 2, far, low)
                start_share(T03, r, rows_of(r))

            first = jnp.where(c == chunks - 2, 0, c)
            stop = jnp.where(c >= chunks - 2, c + 1, 0)
            loop(first, stop, last)
            loop(jnp.maximum(c - 1, 0), c, finish_end)

        loop(0, chunks, take)
        loop(chunks - 1, chunks, finish_end)

        def settled(tile, where):
            return gathered(tile, 0, where) + back_in[(tile,) + where].astype(f32)

        def cross_end(tile, sep):
            def body(c):
                where = rows_of(c)
                total = gathered(tile, c, where)
                give_back(tile, c, where).wait_recv()
                total = total + back_in[(tile,) + where].astype(f32)
                final_out[(sep,) + where] = total.astype(bf16)
                deliver(sep, c).start()

            return body

        give_back(T12, 0, whole).wait_recv()
        out[0] = settled(T12, whole).astype(bf16)
        loop(0, chunks - 1, cross_end(T02, 1))
        give_back(T13, 0, whole).wait_recv()
        out[1] = settled(T13, whole).astype(bf16)
        out[2] = jnp.zeros(out.shape[1:], bf16)
        loop(0, chunks - 1, cross_end(T03, 2))
        loop(chunks - 1, chunks, cross_end(T02, 1))
        loop(chunks - 1, chunks, cross_end(T03, 2))

        send_spec(2, spec, spec1, 2).wait_send()
        mid(high, 2).wait_send()
        loop(0, chunks, lambda c: hop(outer, far, fw_s, fw_r, c, row_chunk(c, high), 2).wait_send())
        for tile, pieces, where_of in (
            (T12, 1, lambda c: whole), (T13, 1, lambda c: whole),
            (T02, chunks, rows_of), (T03, chunks, rows_of), (TEND, chunks, rows_of),
        ):
            settle(tile, pieces, where_of)
        for sep in range(3):
            loop(0, chunks, lambda c: deliver(sep, c).wait_send())

    @pl.when(freq == 2)
    def _():
        mid(low, 1).start()

        def relay(g):
            hop(own, outer, o1_s, o1_r, g, block_chunk(g, low), 2).wait_recv()
            hop(outer, far, fw_s, fw_r, g, block_chunk(g, low), 1).start()

        loop(0, groups, relay)
        send_spec(1, spec, spec0, 2).wait_recv()
        send_spec(2, spec, spec1, 2).wait_recv()
        mid(high, 2).wait_recv()
        loop(0, chunks, lambda c: by_rows(T12, c, near, spec1, 0, own, high))
        start_share(T12, 0, whole)

        def return_rows(tile):
            def body(c):
                where = rows_of(c)
                back_out[(tile,) + where] = gathered(tile, c, where).astype(bf16)
                give_back(tile, c, where).start()

            return body

        def row_product(tile, sep, right):
            def body(c):
                by_rows(tile, c, far, spec0, sep, right, high)
                start_share(tile, c, rows_of(c))

            return body

        def take_columns(g):
            hop(own, outer, o2_s, o2_r, g, block_chunk(g, high), 2).wait_recv()
            by_columns(T13, g, near, spec1, 1, outer, high)
            start_share(T13, g, cols_of(g))
            by_columns(TEND, g, own, spec, 0, outer, full)
            start_share(TEND, g, cols_of(g))

        def return_first():
            back_out[T12] = gathered(T12, 0, whole).astype(bf16)
            give_back(T12, 0, whole).start()

        steps = max(groups, chunks)

        def take(c):
            if groups == steps:
                take_columns(c)
            else:
                loop(c, jnp.minimum(c + 1, groups), take_columns)

            @pl.when(c == 0)
            def _():
                return_first()

            @pl.when(c == steps - 1)
            def _():
                loop(0, chunks - 1, row_product(T03, 2, outer))
                loop(0, groups, return_columns)
                give_back(T13, 0, whole).start()
                loop(0, chunks - 1, return_rows(T03))

            hop(outer, far, fw_s, fw_r, c, row_chunk(c, high), 2).wait_recv()
            row_product(T02, 1, own)(c)

            @pl.when(c == steps - 1)
            def _():
                row_product(T03, 2, outer)(c)

            loop(jnp.maximum(c - 1, 0), c, return_rows(T02))

        def return_columns(g):
            where = cols_of(g)
            back_out[(T13,) + where] = gathered(T13, g, where).astype(bf16)

        loop(0, steps, take)
        loop(chunks - 1, chunks, return_rows(T02))
        loop(chunks - 1, chunks, return_rows(T03))

        def end_columns(g):
            where = cols_of(g)
            out[(0,) + where] = gathered(TEND, g, where).astype(bf16)

        loop(0, groups, end_columns)
        out[1] = jnp.zeros(out.shape[1:], bf16)
        out[2] = jnp.zeros(out.shape[1:], bf16)

        mid(low, 1).wait_send()
        loop(0, groups, lambda g: hop(outer, far, fw_s, fw_r, g, block_chunk(g, low), 1).wait_send())
        for tile, pieces, where_of in (
            (T12, 1, lambda c: whole), (T13, groups, cols_of),
            (T02, chunks, rows_of), (T03, chunks, rows_of), (TEND, groups, cols_of),
        ):
            settle(tile, pieces, where_of)
        give_back(T12, 0, whole).wait_send()
        give_back(T13, 0, whole).wait_send()
        loop(0, chunks, lambda c: give_back(T02, c, rows_of(c)).wait_send())
        loop(0, chunks, lambda c: give_back(T03, c, rows_of(c)).wait_send())


def meet_sums(beam_matrix, sky_spectrum, local_rows):
    _, parts, modes, width = beam_matrix.shape
    separations = sky_spectrum.shape[1]
    groups = modes // local_rows
    tiles = 4 * 2 * local_rows * modes
    block = parts * modes * width
    cut = int(width * (0.5 - tiles / (4 * block))) // LANES * LANES
    pieces = max(CHUNKS, groups)
    bf16 = jnp.bfloat16
    shape = (parts, groups, local_rows, width)
    tile = (2, local_rows, modes)
    dma = pltpu.SemaphoreType.DMA
    pair = lambda *dims: [dma(dims), dma(dims)]
    return pl.pallas_call(
        functools.partial(meet_kernel, cut),
        out_shape=jax.ShapeDtypeStruct((separations,) + tile, bf16),
        in_specs=[pl.BlockSpec(memory_space=pltpu.VMEM)] * 2,
        out_specs=pl.BlockSpec(memory_space=pltpu.VMEM),
        scratch_shapes=[
            pltpu.VMEM(shape, bf16),
            pltpu.VMEM(shape, bf16),
            pltpu.VMEM(shape, bf16),
            pltpu.VMEM(sky_spectrum.shape[1:], jnp.float32),
            pltpu.VMEM(sky_spectrum.shape[1:], jnp.float32),
            pltpu.VMEM((5, groups) + tile, bf16),
            pltpu.VMEM((5, groups - 1) + tile, bf16),
            pltpu.VMEM((4,) + tile, bf16),
            pltpu.VMEM((4,) + tile, bf16),
            pltpu.VMEM((3,) + tile, bf16),
            pltpu.VMEM((3,) + tile, bf16),
            *pair(3), *pair(1), *pair(pieces), *pair(pieces), *pair(pieces),
            *pair(5, pieces, groups - 1), *pair(4, pieces), *pair(3, pieces),
        ],
        compiler_params=pltpu.CompilerParams(
            collective_id=0, has_side_effects=True, vmem_limit_bytes=60 * 2**20
        ),
    )(beam_matrix[0].reshape(shape), sky_spectrum[0])


def local(beam_matrix, sky_spectrum, taper_tiles, noise_tiles):
    per_device, _, modes, width = beam_matrix.shape
    separations = sky_spectrum.shape[1]
    local_rows = taper_tiles.shape[1]
    in_line = (
        per_device == 1
        and separations == 3
        and lax.axis_size("freq") == separations + 1
        and modes // local_rows == CHUNKS
        and local_rows % LANES == 0
        and width % (8 * LANES) == 0
    )
    if in_line:
        summed = meet_sums(beam_matrix, sky_spectrum, local_rows)
        summed = jnp.swapaxes(summed, 1, 2).astype(jnp.float32)
    else:
        summed = general_sums(beam_matrix, sky_spectrum, local_rows)
    summed = summed.reshape(per_device, separations, local_rows, 2, modes)
    taper = taper_tiles.astype(jnp.float32)[None, :, :, None, :]
    return taper * summed + noise_tiles.astype(jnp.float32)


def solution(mesh):
    placed = (
        P(("grp", "freq"), None, None, ("ell", "pol")),
        P(("grp", "freq"), None, ("ell", "pol")),
        P(None, ("ell", "pol"), None),
        P(("grp", "freq"), None, ("ell", "pol"), None, None),
    )
    return jax.shard_map(
        local,
        mesh=mesh,
        in_specs=placed,
        out_specs=P(("grp", "freq"), None, ("ell", "pol"), None, None),
        check_vma=False,
    )
```

```python
import functools

import jax
import jax.numpy as jnp
from jax import lax
from jax.experimental import pallas as pl
from jax.experimental.pallas import tpu as pltpu
from jax.sharding import PartitionSpec as P

CHUNKS = 4
LANES = 128


def passed_along(block, axis, distance):
    devices = range(lax.axis_size(axis))
    route = [(i - distance, i) for i in devices if i - distance in devices]
    return lax.ppermute(block, axis, route)


def general_sums(beam_matrix, sky_spectrum, local_rows):
    per_device = beam_matrix.shape[0]
    mode_count = beam_matrix.shape[2]
    separations = sky_spectrum.shape[1]
    needed = (per_device - 1 + separations) // per_device
    blocks = [beam_matrix]
    for offset in range(needed):
        blocks.append(passed_along(beam_matrix, "freq", -(offset + 1)))
    term_list = []
    for sep_index in range(separations):
        target = sep_index + 1
        partner = blocks[target // per_device][target % per_device]
        spec_row = sky_spectrum[0, sep_index]
        scaled = (spec_row[None, None, :] * beam_matrix[0].astype(jnp.float32)).astype(jnp.bfloat16)
        right = jnp.concatenate([partner[0], partner[1]], axis=-1)
        top = jnp.concatenate([scaled[0], scaled[1]], axis=-1)
        bottom = jnp.concatenate([scaled[1], -scaled[0]], axis=-1)
        left = jnp.stack([top, bottom], axis=1).reshape(2 * mode_count, top.shape[-1])
        product = lax.dot_general(
            left, right, (((1,), (1,)), ((), ())), preferred_element_type=jnp.float32
        ).reshape(mode_count, 2, mode_count)
        term_list.append(
            lax.psum_scatter(
                product.astype(jnp.bfloat16), ("ell", "pol"), scatter_dimension=0, tiled=True
            ).astype(jnp.float32)
        )
    return jnp.stack(term_list)


T12, T13, T02, T03, TEND = range(5)


def meet_kernel(
    cut, own, spec, out,
    outer, near, far, spec0, spec1, stage, inbox, back_out, back_in, final_out, final_in,
    spec_s, spec_r, near_s, near_r, o1_s, o1_r, o2_s, o2_r, fw_s, fw_r,
    rs_s, rs_r, bk_s, bk_r, fn_s, fn_r,
):
    f32, bf16 = jnp.float32, jnp.bfloat16
    _, groups, rows, width = own.shape
    modes = groups * rows
    chunks = CHUNKS
    step = rows // chunks
    freqs = lax.axis_size("freq")
    pols = lax.axis_size("pol")
    freq = lax.axis_index("freq")
    me = lax.axis_index("ell") * pols + lax.axis_index("pol")
    low, high, full = (0, cut), (cut, width), (0, width)
    every = slice(None)

    barrier = pltpu.get_barrier_semaphore()
    for d in range(1, freqs):
        pl.semaphore_signal(
            barrier, inc=1, device_id={"freq": lax.rem(freq + d, freqs)},
            device_id_type=pl.DeviceIdType.MESH,
        )
    for d in range(1, groups):
        other = lax.rem(me + d, groups)
        pl.semaphore_signal(
            barrier, inc=1, device_id={"ell": other // pols, "pol": lax.rem(other, pols)},
            device_id_type=pl.DeviceIdType.MESH,
        )
    pl.semaphore_wait(barrier, freqs - 1 + groups - 1)

    def span(c):
        return pl.ds(pl.multiple_of(c * step, step), step)

    def to_freq(src, dst, send, recv, target):
        return pltpu.make_async_remote_copy(
            src_ref=src, dst_ref=dst, send_sem=send, recv_sem=recv,
            device_id={"freq": target}, device_id_type=pl.DeviceIdType.MESH,
        )

    def lanes(part):
        return pl.ds(part[0], part[1] - part[0])

    def send_spec(n, src, dst, target):
        return to_freq(src, dst, spec_s.at[n], spec_r.at[n], target)

    def mid(part, target):
        where = (every, every, every, lanes(part))
        return to_freq(own.at[where], near.at[where], near_s.at[0], near_r.at[0], target)

    def row_chunk(c, part):
        return (every, every, span(c), lanes(part))

    def block_chunk(g, part):
        return (every, pl.ds(g, 1), every, lanes(part))

    def hop(src, dst, send, recv, c, where, target):
        return to_freq(src.at[where], dst.at[where], send.at[c], recv.at[c], target)

    def share(tile, piece, where):
        copies = []
        for d in range(1, groups):
            other = lax.rem(me + d, groups)
            copies.append(
                pltpu.make_async_remote_copy(
                    src_ref=stage.at[(tile, other) + where],
                    dst_ref=inbox.at[(tile, d - 1) + where],
                    send_sem=rs_s.at[tile, piece, d - 1],
                    recv_sem=rs_r.at[tile, piece, d - 1],
                    device_id={"ell": other // pols, "pol": lax.rem(other, pols)},
                    device_id_type=pl.DeviceIdType.MESH,
                )
            )
        return copies

    def start_share(tile, piece, where):
        for copy in share(tile, piece, where):
            copy.start()

    whole = (every, every, every)

    def rows_of(c):
        return (every, span(c), every)

    def cols_of(g):
        return (every, every, pl.ds(pl.multiple_of(g * rows, rows), rows))

    def dot(a, b):
        return lax.dot_general(a, b, (((1,), (1,)), ((), ())), preferred_element_type=f32)

    def scaled(block, part_index, where, weight):
        value = block[(part_index,) + where].reshape(-1, weight.shape[-1])
        return (weight * value.astype(f32)).astype(bf16)

    def cross(left, left_where, weight, right, right_where):
        a_re = scaled(left, 0, left_where, weight)
        a_im = scaled(left, 1, left_where, weight)
        b_re = right[(0,) + right_where].reshape(-1, weight.shape[-1])
        b_im = right[(1,) + right_where].reshape(-1, weight.shape[-1])
        real = dot(a_re, b_re) + dot(a_im, b_im)
        imag = dot(a_im, b_re) - dot(a_re, b_im)
        return real.astype(bf16), imag.astype(bf16)

    def by_rows(tile, c, left, weights, sep, right, part):
        weight = weights[pl.ds(sep, 1), lanes(part)]
        real, imag = cross(
            left, (every, span(c), lanes(part)), weight, right, (every, every, lanes(part))
        )
        stage[tile, :, 0, span(c), :] = real.reshape(groups, step, modes)
        stage[tile, :, 1, span(c), :] = imag.reshape(groups, step, modes)

    def by_columns(tile, g, left, weights, sep, right, part):
        weight = weights[pl.ds(sep, 1), lanes(part)]
        columns = pl.ds(pl.multiple_of(g * rows, rows), rows)

        def body(o, carry):
            real, imag = cross(
                left, (o, every, lanes(part)), weight, right, (g, every, lanes(part))
            )
            stage[tile, o, 0, :, columns] = real
            stage[tile, o, 1, :, columns] = imag
            return carry

        lax.fori_loop(0, groups, body, 0)

    def gathered(tile, piece, where):
        for copy in share(tile, piece, where):
            copy.wait_recv()
        total = stage[(tile, me) + where].astype(f32)
        for d in range(groups - 1):
            total = total + inbox[(tile, d) + where].astype(f32)
        return total

    def loop(lo, hi, body):
        def wrapped(i, carry):
            body(i)
            return carry

        lax.fori_loop(lo, hi, wrapped, 0)

    def settle(tile, pieces, where_of):
        def body(c):
            for copy in share(tile, c, where_of(c)):
                copy.wait_send()

        loop(0, pieces, body)

    def give_back(tile, c, where):
        return to_freq(
            back_out.at[(tile,) + where], back_in.at[(tile,) + where],
            bk_s.at[tile, c], bk_r.at[tile, c], 0 if tile in (T02, T03) else 1,
        )

    def deliver(sep, c):
        where = rows_of(c)
        return to_freq(
            final_out.at[(sep,) + where], final_in.at[(sep,) + where],
            fn_s.at[sep, c], fn_r.at[sep, c], 0,
        )

    @pl.when(freq == 0)
    def _():
        send_spec(0, spec, spec0, 1).start()
        send_spec(1, spec, spec0, 2).start()
        loop(0, chunks, lambda c: hop(own, outer, o1_s, o1_r, c, row_chunk(c, high), 1).start())
        loop(0, chunks, lambda c: hop(own, outer, o2_s, o2_r, c, row_chunk(c, low), 1).start())
        send_spec(0, spec, spec0, 1).wait_send()
        send_spec(1, spec, spec0, 2).wait_send()
        loop(0, chunks, lambda c: hop(own, outer, o1_s, o1_r, c, row_chunk(c, high), 1).wait_send())
        loop(0, chunks, lambda c: hop(own, outer, o2_s, o2_r, c, row_chunk(c, low), 1).wait_send())

        def land(c):
            for sep, tile in ((1, T02), (2, T03)):
                where = rows_of(c)
                deliver(sep, c).wait_recv()
                give_back(tile, c, where).wait_recv()
                total = final_in[(sep,) + where].astype(f32) + back_in[(tile,) + where].astype(f32)
                out[(sep,) + where] = total.astype(bf16)

        loop(0, chunks, lambda c: deliver(0, c).wait_recv())
        out[0] = final_in[0]
        loop(0, chunks, land)

    @pl.when(freq == 3)
    def _():
        loop(0, groups, lambda g: hop(own, outer, o1_s, o1_r, g, block_chunk(g, low), 2).start())
        loop(0, groups, lambda g: hop(own, outer, o2_s, o2_r, g, block_chunk(g, high), 2).start())
        out[...] = jnp.zeros_like(out)
        loop(0, groups, lambda g: hop(own, outer, o1_s, o1_r, g, block_chunk(g, low), 2).wait_send())
        loop(0, groups, lambda g: hop(own, outer, o2_s, o2_r, g, block_chunk(g, high), 2).wait_send())

    @pl.when(freq == 1)
    def _():
        send_spec(2, spec, spec1, 2).start()
        mid(high, 2).start()

        def relay(c):
            hop(own, outer, o1_s, o1_r, c, row_chunk(c, high), 1).wait_recv()
            hop(outer, far, fw_s, fw_r, c, row_chunk(c, high), 2).start()

        loop(0, chunks - 1, relay)
        mid(low, 1).wait_recv()
        loop(0, chunks, lambda c: by_rows(T12, c, own, spec, 0, near, low))
        start_share(T12, 0, whole)
        loop(chunks - 1, chunks, relay)
        send_spec(0, spec, spec0, 1).wait_recv()

        def finish_end(c):
            final_out[(0,) + rows_of(c)] = gathered(TEND, c, rows_of(c)).astype(bf16)
            deliver(0, c).start()

        def cross_end(tile, sep):
            def body(c):
                where = rows_of(c)
                final_out[(sep,) + where] = gathered(tile, c, where).astype(bf16)
                deliver(sep, c).start()

            return body

        def block_in(g):
            hop(outer, far, fw_s, fw_r, g, block_chunk(g, low), 1).wait_recv()

        def columns_end(g):
            by_columns(T13, g, own, spec, 1, far, low)
            start_share(T13, g, cols_of(g))

        def near_end(g):
            block_in(g)
            columns_end(g)

        def take(c):
            hop(own, outer, o2_s, o2_r, c, row_chunk(c, low), 1).wait_recv()
            by_rows(TEND, c, outer, spec0, 0, own, full)
            start_share(TEND, c, rows_of(c))
            by_rows(T02, c, outer, spec0, 1, near, low)
            start_share(T02, c, rows_of(c))

            def last(r):
                by_rows(T03, r, outer, spec0, 2, far, low)
                start_share(T03, r, rows_of(r))

            first = jnp.where(c == chunks - 2, 0, c)
            stop = jnp.where(c >= chunks - 2, c + 1, 0)
            loop(c, jnp.where(c < chunks - 2, c + 1, c), near_end)
            loop(chunks - 2, jnp.where(c == chunks - 2, chunks, 0), block_in)
            loop(first, stop, last)
            before = jnp.maximum(c - 1, 0)
            loop(before, c, finish_end)
            loop(before, c, cross_end(T02, 1))
            loop(0, jnp.where(c == chunks - 1, c, 0), cross_end(T03, 2))

        loop(0, chunks, take)
        loop(chunks - 2, chunks, columns_end)
        loop(chunks - 1, chunks, finish_end)

        loop(chunks - 1, chunks, cross_end(T02, 1))
        loop(chunks - 1, chunks, cross_end(T03, 2))
        out[2] = jnp.zeros(out.shape[1:], bf16)
        give_back(T12, 0, whole).wait_recv()
        total = gathered(T12, 0, whole) + back_in[T12].astype(f32)
        out[0] = total.astype(bf16)
        give_back(T13, 0, whole).wait_recv()

        def own_columns(g):
            where = cols_of(g)
            total = gathered(T13, g, where) + back_in[(T13,) + where].astype(f32)
            out[(1,) + where] = total.astype(bf16)

        loop(0, groups, own_columns)

        send_spec(2, spec, spec1, 2).wait_send()
        mid(high, 2).wait_send()
        loop(0, chunks, lambda c: hop(outer, far, fw_s, fw_r, c, row_chunk(c, high), 2).wait_send())
        for tile, pieces, where_of in (
            (T12, 1, lambda c: whole), (T13, groups, cols_of),
            (T02, chunks, rows_of), (T03, chunks, rows_of), (TEND, chunks, rows_of),
        ):
            settle(tile, pieces, where_of)
        for sep in range(3):
            loop(0, chunks, lambda c: deliver(sep, c).wait_send())

    @pl.when(freq == 2)
    def _():
        mid(low, 1).start()

        def relay(g):
            hop(own, outer, o1_s, o1_r, g, block_chunk(g, low), 2).wait_recv()
            hop(outer, far, fw_s, fw_r, g, block_chunk(g, low), 1).start()

        loop(0, groups, relay)
        send_spec(1, spec, spec0, 2).wait_recv()
        send_spec(2, spec, spec1, 2).wait_recv()
        mid(high, 2).wait_recv()
        loop(0, chunks, lambda c: by_rows(T12, c, near, spec1, 0, own, high))
        start_share(T12, 0, whole)

        def return_rows(tile):
            def body(c):
                where = rows_of(c)
                back_out[(tile,) + where] = gathered(tile, c, where).astype(bf16)
                give_back(tile, c, where).start()

            return body

        def row_product(tile, sep, right):
            def body(c):
                by_rows(tile, c, far, spec0, sep, right, high)
                start_share(tile, c, rows_of(c))

            return body

        def end_product(g):
            by_columns(TEND, g, own, spec, 0, outer, full)
            start_share(TEND, g, cols_of(g))

        def take_columns(g):
            hop(own, outer, o2_s, o2_r, g, block_chunk(g, high), 2).wait_recv()
            by_columns(T13, g, near, spec1, 1, outer, high)
            start_share(T13, g, cols_of(g))
            loop(g, jnp.minimum(g + 1, groups - 1), end_product)

        per = chunks // groups
        late = chunks - per

        def take(c):
            due = jnp.where(lax.rem(c, per) == 0, 1, 0)
            loop(c // per, c // per + due, take_columns)

            @pl.when(c == 0)
            def _():
                back_out[T12] = gathered(T12, 0, whole).astype(bf16)
                give_back(T12, 0, whole).start()

            @pl.when(c == late)
            def _():
                loop(0, late, row_product(T03, 2, outer))
                loop(0, groups, return_columns)
                give_back(T13, 0, whole).start()

            hop(outer, far, fw_s, fw_r, c, row_chunk(c, high), 2).wait_recv()
            row_product(T02, 1, own)(c)
            loop(c, jnp.where(c >= late, c + 1, c), row_product(T03, 2, outer))
            loop(jnp.maximum(c - 1, 0), c, return_rows(T02))
            loop(jnp.where(c == late, 0, jnp.maximum(c - 1, 0)), jnp.where(c >= late, c, 0), return_rows(T03))

        def return_columns(g):
            where = cols_of(g)
            back_out[(T13,) + where] = gathered(T13, g, where).astype(bf16)

        loop(0, chunks, take)
        loop(groups - 1, groups, end_product)
        loop(chunks - 1, chunks, return_rows(T02))
        loop(chunks - 1, chunks, return_rows(T03))

        def end_columns(g):
            where = cols_of(g)
            out[(0,) + where] = gathered(TEND, g, where).astype(bf16)

        loop(0, groups, end_columns)
        out[1] = jnp.zeros(out.shape[1:], bf16)
        out[2] = jnp.zeros(out.shape[1:], bf16)

        mid(low, 1).wait_send()
        loop(0, groups, lambda g: hop(outer, far, fw_s, fw_r, g, block_chunk(g, low), 1).wait_send())
        for tile, pieces, where_of in (
            (T12, 1, lambda c: whole), (T13, groups, cols_of),
            (T02, chunks, rows_of), (T03, chunks, rows_of), (TEND, groups, cols_of),
        ):
            settle(tile, pieces, where_of)
        give_back(T12, 0, whole).wait_send()
        give_back(T13, 0, whole).wait_send()
        loop(0, chunks, lambda c: give_back(T02, c, rows_of(c)).wait_send())
        loop(0, chunks, lambda c: give_back(T03, c, rows_of(c)).wait_send())


def meet_sums(beam_matrix, sky_spectrum, local_rows):
    _, parts, modes, width = beam_matrix.shape
    separations = sky_spectrum.shape[1]
    groups = modes // local_rows
    tiles = 4 * 2 * local_rows * modes
    block = parts * modes * width
    cut = int(width * (0.5 - tiles / (4 * block))) // LANES * LANES
    pieces = max(CHUNKS, groups)
    bf16 = jnp.bfloat16
    shape = (parts, groups, local_rows, width)
    tile = (2, local_rows, modes)
    dma = pltpu.SemaphoreType.DMA
    pair = lambda *dims: [dma(dims), dma(dims)]
    return pl.pallas_call(
        functools.partial(meet_kernel, cut),
        out_shape=jax.ShapeDtypeStruct((separations,) + tile, bf16),
        in_specs=[pl.BlockSpec(memory_space=pltpu.VMEM)] * 2,
        out_specs=pl.BlockSpec(memory_space=pltpu.VMEM),
        scratch_shapes=[
            pltpu.VMEM(shape, bf16),
            pltpu.VMEM(shape, bf16),
            pltpu.VMEM(shape, bf16),
            pltpu.VMEM(sky_spectrum.shape[1:], jnp.float32),
            pltpu.VMEM(sky_spectrum.shape[1:], jnp.float32),
            pltpu.VMEM((5, groups) + tile, bf16),
            pltpu.VMEM((5, groups - 1) + tile, bf16),
            pltpu.VMEM((4,) + tile, bf16),
            pltpu.VMEM((4,) + tile, bf16),
            pltpu.VMEM((3,) + tile, bf16),
            pltpu.VMEM((3,) + tile, bf16),
            *pair(3), *pair(1), *pair(pieces), *pair(pieces), *pair(pieces),
            *pair(5, pieces, groups - 1), *pair(4, pieces), *pair(3, pieces),
        ],
        compiler_params=pltpu.CompilerParams(
            collective_id=0, has_side_effects=True, vmem_limit_bytes=60 * 2**20
        ),
    )(beam_matrix[0].reshape(shape), sky_spectrum[0])


def local(beam_matrix, sky_spectrum, taper_tiles, noise_tiles):
    per_device, _, modes, width = beam_matrix.shape
    separations = sky_spectrum.shape[1]
    local_rows = taper_tiles.shape[1]
    in_line = (
        per_device == 1
        and separations == 3
        and lax.axis_size("freq") == separations + 1
        and modes // local_rows == CHUNKS
        and local_rows % LANES == 0
        and width % (8 * LANES) == 0
    )
    if in_line:
        summed = meet_sums(beam_matrix, sky_spectrum, local_rows)
        summed = jnp.swapaxes(summed, 1, 2).astype(jnp.float32)
    else:
        summed = general_sums(beam_matrix, sky_spectrum, local_rows)
    summed = summed.reshape(per_device, separations, local_rows, 2, modes)
    taper = taper_tiles.astype(jnp.float32)[None, :, :, None, :]
    return taper * summed + noise_tiles.astype(jnp.float32)


def solution(mesh):
    placed = (
        P(("grp", "freq"), None, None, ("ell", "pol")),
        P(("grp", "freq"), None, ("ell", "pol")),
        P(None, ("ell", "pol"), None),
        P(("grp", "freq"), None, ("ell", "pol"), None, None),
    )
    return jax.shard_map(
        local,
        mesh=mesh,
        in_specs=placed,
        out_specs=P(("grp", "freq"), None, ("ell", "pol"), None, None),
        check_vma=False,
    )
```
